512 devices in a mesh: chain: 2 (over core), sector: 256 (over z, y, x).
Axes of the slice: x: 4, y: 8, z: 8, core: 2. Of those that a mesh axis runs over, the one named last changes fastest.
Arguments:
- env_first: bfloat16 [2, 256, 15, 128, 128], P(None, 'sector'), may hold values from -6 to 6
- states: bfloat16 [2, 2, 4, 256, 128, 128], P('chain', None, None, 'sector'), may hold values from -0.5 to 0.5
- mpo: bfloat16 [2, 4, 15, 15], P('chain'), may hold values from -1.5 to 1.5
- block_rows: int32 [2, 256], P('chain', 'sector'), may hold values from 1 to 128, 16384 in all within a row
- present: int32 [2, 4, 256], P('chain', None, 'sector'), may hold values 0 or 1
Outputs:
- env_out: bfloat16 [2, 2, 256, 15, 128, 128], P('chain', None, 'sector')
The draws below stay inside these ranges and needn't reach their ends.
Inputs may be any that keep to these rules, and one draw needn't show every extreme that they name: `block_rows`: in each site's row the 256 live sizes add up to 16384, and one of them equals 128.
All inputs are finite; a program needn't handle non-finite values. No bound on the sum of `block_rows` or of `present` on one device may be relied on, other than what follows from the above.
Results may differ from the reference program's by a relative error of at most 0.008.
Values may be sent and summed in bfloat16 or wider, within the bound.
A program may use at most 128 MiB of HBM per device.

```python
import math
import jax
import jax.numpy as jnp
import numpy as np
from jax import lax

BLK = 128
W = 15
D_PHYS = 4
TARGETS = 2
QD = 4
SECTORS = 256
SITES = 2


def place_ends(array, key, smallest, largest):
    place = [jax.random.randint(jax.random.fold_in(key, axis), (), 0, length) for axis, length in enumerate(array.shape)]
    widest = array.shape.index(max(array.shape))
    next_to = place[:widest] + [(place[widest] + 1) % array.shape[widest]] + place[widest + 1:]
    return array.at[tuple(place)].set(smallest).at[tuple(next_to)].set(largest)


def shard_levels(own_key, shape, shards, smallest, top_value):
    level, own = 1.0, jax.random.fold_in(own_key, 6)
    for position, parts in shards:
        steps = jnp.exp(jax.random.uniform(jax.random.fold_in(own, position), (parts,), jnp.float32, smallest / len(shards), top_value / len(shards)))
        level = level * jnp.repeat(steps, shape[position] // parts).reshape([-1 if axis == position else 1 for axis in range(len(shape))])
    return level


def split_up(amount, total, limit, lean):
    weights = [(1 << 20) // math.isqrt(grade ** lean) + 1 for grade in range(2, amount + 1)]
    rest, holding = total - limit - (amount - 1), [1] * (amount - 1)
    while rest > 0:
        free = [i for i in range(amount - 1) if holding[i] < limit]
        pool, left = sum([weights[i] for i in free]), rest
        for i in free:
            more = min(limit - holding[i], max(1, left * weights[i] // pool), rest)
            holding[i] = holding[i] + more
            rest = rest - more
    return np.array([limit] + holding)


def uneven_parts(key, number_of, total, most, lean):
    if number_of == 2:
        one = jax.random.randint(key, (), max(1, total - most), min(most, total - 1) + 1)
        return jnp.stack([one, total - one])
    lengths = jnp.asarray(split_up(number_of, total, most, lean), jnp.int32)
    pairs = (number_of - 1) // 2
    donor, sink = lengths[1:1 + 2 * pairs:2], lengths[2:2 + 2 * pairs:2]
    margin = jnp.minimum(donor - 1, most - sink)
    passed = jax.random.randint(jax.random.fold_in(key, 1), (pairs,), 0, 1 << 20) % (margin + 1)
    lengths = lengths.at[1:1 + 2 * pairs:2].set(donor - passed).at[2:2 + 2 * pairs:2].set(sink + passed)
    return lengths[jax.random.permutation(jax.random.fold_in(key, 2), number_of)]


def centred(rng, dims, deviation, bound, split=(), kind=jnp.bfloat16):
    gain = shard_levels(rng, dims, split, -0.22, 0.18) if split else 1.0
    entries = jax.random.normal(rng, dims, jnp.float32) * deviation * gain
    return jnp.minimum(jnp.maximum(entries, -bound), bound).astype(kind)


def setup_inputs(seed: int = 0) -> dict:
    streams_of = jax.random.split(jax.random.key(seed), 6)
    return {
        "env_first": centred(streams_of[0], (TARGETS, SECTORS, W, BLK, BLK), 1.0, 6.0, ((1, 256),)),
        "states": centred(streams_of[1], (SITES, TARGETS, D_PHYS, SECTORS, BLK, BLK), BLK ** -0.5, 0.5, ((0, 2), (3, 256))),
        "mpo": centred(streams_of[2], (SITES, D_PHYS, W, W), W ** -0.5, 1.5, ((0, 2),)),
        "block_rows": jax.vmap(lambda own: uneven_parts(own, SECTORS, SECTORS * BLK // 2, BLK, 2))(jax.random.split(streams_of[3], SITES)).reshape((SITES, SECTORS)).astype(jnp.int32),
        "present": place_ends((jax.random.randint(streams_of[4], (SITES, D_PHYS, SECTORS), 0, 4) < 3).astype(jnp.int32), jax.random.fold_in(streams_of[4], 1), 0, 1),
    }


def shift_sectors(values, offset):
    sector_count = values.shape[1]
    return jnp.concatenate([jnp.zeros_like(values[:, :offset]), values[:, :sector_count - offset]], axis=1)


def reference(env_first, states, mpo, block_rows, present):
    environment = env_first
    sector_ids = jnp.arange(SECTORS)
    inside_grid = (sector_ids % QD < QD - 1).astype(jnp.float32)
    state_ids = jnp.arange(D_PHYS)
    collected = []
    for site_index in range(SITES):
        blocks = states[site_index].astype(jnp.float32)
        projected = jnp.einsum("tkwab,tskbc->tskwac", environment.astype(jnp.float32), blocks).astype(jnp.bfloat16)
        projected = lax.optimization_barrier(projected).astype(jnp.float32)
        sandwich = jnp.einsum("tskad,tskwac->tskwdc", blocks, projected)
        coupled = jnp.einsum("tskwdc,swv->tskvdc", sandwich, mpo[site_index].astype(jnp.float32), precision=lax.Precision.HIGHEST)
        keep_mask = present[site_index].astype(jnp.float32) * jnp.where(state_ids[:, None] >= 2, inside_grid[None, :], 1.0)
        partials = (coupled * keep_mask[None, :, :, None, None, None]).astype(jnp.bfloat16)
        partials = lax.optimization_barrier(partials).astype(jnp.float32)
        summed = partials[:, 0] + shift_sectors(partials[:, 2], 1) + shift_sectors(partials[:, 1], QD) + shift_sectors(partials[:, 3], QD + 1)
        live_rows = jnp.arange(BLK)[None, :] < block_rows[site_index][:, None]
        live_mask = live_rows[:, None, :, None] & live_rows[:, None, None, :]
        environment = jnp.where(live_mask[None], summed, 0.0).astype(jnp.bfloat16)
        collected.append(environment)
    return jnp.stack(collected)
```

```python
import jax
import jax.numpy as jnp
from jax import lax
from jax.experimental import pallas as pl
from jax.experimental.pallas import tpu as pltpu
from jax.sharding import PartitionSpec as P

QD = 4
W = 15
BLK = 128
SUB = 16
CHUNK = 5
CHUNKS = W // CHUNK
MESH = pl.DeviceIdType.MESH
BF = jnp.bfloat16
F32 = jnp.float32


def kernel(
    env_in, states_in, pack_in, out,
    env, blocks, pack, joined, turned, kron, proj, mixed, parts, got,
    env_sem, own_sem, part_send, part_recv, swap_send, swap_recv, out_sem, out_send, out_recv,
):
    sectors = lax.axis_size("sector")
    core, k = lax.axis_index("chain"), lax.axis_index("sector")
    other = 1 - core
    down = lax.rem(k, QD)
    goes_right, comes_left = down < QD - 1, down > 0
    goes_up, comes_below = k < sectors - QD, k >= QD
    routes = {
        1: (QD, goes_up, comes_below),
        2: (1, goes_right, comes_left),
        3: (QD + 1, goes_right & goes_up, comes_left & comes_below),
    }

    env_copies = [
        pltpu.make_async_copy(
            env_in.at[core, 0, pl.ds(c * CHUNK, CHUNK)], env.at[0, pl.ds(c * CHUNK, CHUNK)], env_sem.at[c]
        )
        for c in range(CHUNKS)
    ]
    own_blocks = pltpu.make_async_copy(states_in.at[0, core, :, 0], blocks.at[core], own_sem.at[0])
    own_pack = pltpu.make_async_copy(pack_in, pack.at[core], own_sem.at[1])
    own_blocks.start()
    own_pack.start()
    for copy in env_copies:
        copy.start()

    barrier = pltpu.get_barrier_semaphore()
    pl.semaphore_signal(barrier, inc=1, device_id=(other, k), device_id_type=MESH)
    for step, sends, receives in routes.values():
        @pl.when(sends)
        def _():
            pl.semaphore_signal(barrier, inc=1, device_id=(core, k + step), device_id_type=MESH)

        @pl.when(receives)
        def _():
            pl.semaphore_signal(barrier, inc=1, device_id=(core, k - step), device_id_type=MESH)

    peers = 1
    for step, sends, receives in routes.values():
        peers = peers + sends.astype(jnp.int32) + receives.astype(jnp.int32)
    pl.semaphore_wait(barrier, peers)

    swaps = [
        pltpu.make_async_remote_copy(
            src_ref=source, dst_ref=target, send_sem=swap_send.at[i], recv_sem=swap_recv.at[i],
            device_id=(other, k), device_id_type=MESH,
        )
        for i, (source, target) in enumerate(
            [(pack_in, pack.at[core]), (states_in.at[0, other, :, 0], blocks.at[core])]
        )
    ]
    for swap in swaps:
        swap.start()

    proj[W] = jnp.zeros((BLK, 4 * BLK), BF)
    for s, (step, sends, receives) in routes.items():
        @pl.when(jnp.logical_not(receives))
        def _():
            for site in range(2):
                got[site, s - 1] = jnp.zeros((W, BLK, BLK), BF)

    def await_site(site):
        @pl.when(core == site)
        def _():
            own_blocks.wait()
            own_pack.wait()

        @pl.when(core != site)
        def _():
            for swap in swaps:
                swap.wait_recv()

    def prepare(site):
        spread = (lax.broadcasted_iota(jnp.int32, (W * SUB, SUB), 0) >> 4) == lax.broadcasted_iota(
            jnp.int32, (W * SUB, SUB), 1
        )
        spread = jnp.where(spread, 1.0, 0.0).astype(BF)
        widen = lax.broadcasted_iota(jnp.int32, (BLK, 256), 0) == (
            lax.broadcasted_iota(jnp.int32, (BLK, 256), 1) >> 4
        )
        widen = jnp.where(widen, 1.0, 0.0).astype(BF)
        same = (lax.broadcasted_iota(jnp.int32, (W * SUB, 256), 0) & 15) == (
            lax.broadcasted_iota(jnp.int32, (W * SUB, 256), 1) & 15
        )
        for s in range(4):
            tall = jnp.dot(spread, pack[site, s], preferred_element_type=F32).astype(BF)
            wide = jnp.dot(tall, widen, preferred_element_type=F32)
            kron[s] = jnp.where(same, wide, 0.0).astype(BF)
            block = blocks[site, s]
            joined[:, s * BLK:(s + 1) * BLK] = block
            turned[s] = block.astype(F32).T.astype(BF)

    def project(site, c):
        rows = env[site, c * CHUNK:(c + 1) * CHUNK].reshape(CHUNK * BLK, BLK)
        product = jnp.dot(rows, joined[...], preferred_element_type=F32).astype(BF)
        proj[c * CHUNK:(c + 1) * CHUNK] = product.reshape(CHUNK, BLK, 4 * BLK)

    def part_copy(site, s, c):
        step = routes[s][0]
        span = pl.ds(c * CHUNK, CHUNK)
        return pltpu.make_async_remote_copy(
            src_ref=parts.at[site, s, span], dst_ref=got.at[site, s - 1, span],
            send_sem=part_send.at[site, s - 1, c], recv_sem=part_recv.at[site, s - 1, c],
            device_id=(core, k + step), device_id_type=MESH,
        )

    def mix_and_send(site, s):
        lanes = slice(s * BLK, (s + 1) * BLK)
        for i in range(BLK // (2 * SUB)):
            low, mid, high = 2 * i * SUB, (2 * i + 1) * SUB, (2 * i + 2) * SUB
            right = jnp.concatenate(
                [proj[:, low:mid, lanes].reshape(256, BLK), proj[:, mid:high, lanes].reshape(256, BLK)], axis=1
            )
            product = jnp.dot(kron[s], right, preferred_element_type=F32).astype(BF)
            for v in range(W):
                mixed[low:mid, v * BLK:(v + 1) * BLK] = product[v * SUB:(v + 1) * SUB, :BLK]
                mixed[mid:high, v * BLK:(v + 1) * BLK] = product[v * SUB:(v + 1) * SUB, BLK:]
        for c in range(CHUNKS):
            product = jnp.dot(
                turned[s], mixed[:, c * CHUNK * BLK:(c + 1) * CHUNK * BLK], preferred_element_type=F32
            ).astype(BF)
            for v in range(CHUNK):
                parts[site, s, c * CHUNK + v] = product[:, v * BLK:(v + 1) * BLK]
            if s:
                @pl.when(routes[s][1])
                def _():
                    part_copy(site, s, c).start()

    def out_copies(site, c):
        span = pl.ds(c * CHUNK, CHUNK)
        source, target = env.at[site + 1, span], out.at[0, core, 0, span]
        local = pltpu.make_async_copy(source, target, out_sem.at[c])
        remote = pltpu.make_async_remote_copy(
            src_ref=source, dst_ref=target, send_sem=out_send.at[c], recv_sem=out_recv.at[c],
            device_id=(other, k), device_id_type=MESH,
        )
        return local, remote

    def combine(site, c):
        for s, (step, sends, receives) in routes.items():
            @pl.when(receives)
            def _():
                part_copy(site, s, c).wait_recv()

        size = pack[site, 4].astype(F32)[0:1]
        live = (lax.broadcasted_iota(jnp.int32, (BLK, BLK), 0).astype(F32) < size) & (
            lax.broadcasted_iota(jnp.int32, (BLK, BLK), 1).astype(F32) < size
        )
        for v in range(c * CHUNK, (c + 1) * CHUNK):
            total = parts[site, 0, v].astype(F32) + got[site, 1, v].astype(F32)
            total = total + got[site, 0, v].astype(F32) + got[site, 2, v].astype(F32)
            env[site + 1, v] = jnp.where(live, total, 0.0).astype(BF)
        local, remote = out_copies(site, c)

        @pl.when(core == site)
        def _():
            local.start()

        @pl.when(core != site)
        def _():
            remote.start()

    for site in range(2):
        await_site(site)
        prepare(site)
        for c in range(CHUNKS):
            if site == 0:
                env_copies[c].wait()
            else:
                combine(0, c)
            project(site, c)
        for s in (3, 2, 1, 0):
            mix_and_send(site, s)
    for c in range(CHUNKS):
        combine(1, c)

    for swap in swaps:
        swap.wait_send()
    for site in range(2):
        for s, (step, sends, receives) in routes.items():
            @pl.when(sends)
            def _():
                for c in range(CHUNKS):
                    part_copy(site, s, c).wait_send()
    for site in range(2):
        for c in range(CHUNKS):
            local, remote = out_copies(site, c)

            @pl.when(core == site)
            def _():
                local.wait()
                remote.wait_recv()

            @pl.when(core != site)
            def _():
                remote.wait_send()


def on_device(env_first, states, mpo, block_rows, present):
    down_charge = lax.axis_index("sector") % QD
    inside = jnp.where(jnp.arange(4) >= 2, (down_charge < QD - 1).astype(F32), 1.0)
    keep = present[0, :, 0].astype(F32) * inside
    coupling = jnp.swapaxes(mpo[0], 1, 2).astype(F32) * keep[:, None, None]
    coupling = jnp.pad(coupling, ((0, 0), (0, SUB - W), (0, BLK - W)))
    size = jnp.broadcast_to(block_rows[0, 0].astype(F32), (1, SUB, BLK))
    pack = jnp.concatenate([coupling, size], axis=0).astype(BF)
    anywhere = pl.BlockSpec(memory_space=pl.ANY)
    return pl.pallas_call(
        kernel,
        out_shape=jax.ShapeDtypeStruct((1, 2, 1, W, BLK, BLK), BF),
        in_specs=[anywhere] * 3,
        out_specs=anywhere,
        scratch_shapes=[
            pltpu.VMEM((3, W, BLK, BLK), BF),
            pltpu.VMEM((2, 4, BLK, BLK), BF),
            pltpu.VMEM((2, 5, SUB, BLK), BF),
            pltpu.VMEM((BLK, 4 * BLK), BF),
            pltpu.VMEM((4, BLK, BLK), BF),
            pltpu.VMEM((4, W * SUB, 256), BF),
            pltpu.VMEM((W + 1, BLK, 4 * BLK), BF),
            pltpu.VMEM((BLK, W * BLK), BF),
            pltpu.VMEM((2, 4, W, BLK, BLK), BF),
            pltpu.VMEM((2, 3, W, BLK, BLK), BF),
            pltpu.SemaphoreType.DMA((CHUNKS,)),
            pltpu.SemaphoreType.DMA((2,)),
            pltpu.SemaphoreType.DMA((2, 3, CHUNKS)),
            pltpu.SemaphoreType.DMA((2, 3, CHUNKS)),
            pltpu.SemaphoreType.DMA((2,)),
            pltpu.SemaphoreType.DMA((2,)),
            pltpu.SemaphoreType.DMA((CHUNKS,)),
            pltpu.SemaphoreType.DMA((CHUNKS,)),
            pltpu.SemaphoreType.DMA((CHUNKS,)),
        ],
        compiler_params=pltpu.CompilerParams(
            collective_id=0, has_side_effects=True, vmem_limit_bytes=48 * 1024 * 1024
        ),
    )(env_first, states, pack)


def solution(mesh):
    placed = (
        P(None, "sector", None, None, None),
        P("chain", None, None, "sector", None, None),
        P("chain", None, None, None),
        P("chain", "sector"),
        P("chain", None, "sector"),
    )
    return jax.shard_map(
        on_device,
        mesh=mesh,
        in_specs=placed,
        out_specs=P("chain", None, "sector", None, None, None),
        check_vma=False,
    )
```

```python
import jax
import jax.numpy as jnp
from jax import lax
from jax.experimental import pallas as pl
from jax.experimental.pallas import tpu as pltpu
from jax.sharding import PartitionSpec as P

QD = 4
W = 15
BLK = 128
SUB = 16
SPANS = ((0, 4), (4, 4), (8, 4), (12, 3))
CHUNKS = len(SPANS)
RIGHT_FIRST = (0, 1)
MESH = pl.DeviceIdType.MESH
BF = jnp.bfloat16
F32 = jnp.float32


def kernel(
    env_in, states_in, pack_in, out,
    env, blocks, pack, joined, turned, kron, proj, mixed, parts, got,
    env_sem, own_sem, part_send, part_recv, swap_send, swap_recv, out_sem, out_send, out_recv,
):
    sectors = lax.axis_size("sector")
    core, k = lax.axis_index("chain"), lax.axis_index("sector")
    other = 1 - core
    down = lax.rem(k, QD)
    goes_right, comes_left = down < QD - 1, down > 0
    goes_up, comes_below = k < sectors - QD, k >= QD
    peers_at = ((QD, goes_up, comes_below), (1, goes_right, comes_left))

    def route(slot, c):
        if slot == 0:
            return 1, QD, goes_up, comes_below
        if slot == 1:
            return 2, 1, goes_right, comes_left
        if c in RIGHT_FIRST:
            return 3, 1, goes_right & goes_up, comes_left & goes_up
        return 3, QD, goes_right & goes_up, comes_below & goes_right

    env_copies = [
        pltpu.make_async_copy(
            env_in.at[core, 0, pl.ds(*SPANS[c])], env.at[0, pl.ds(*SPANS[c])], env_sem.at[c]
        )
        for c in range(CHUNKS)
    ]
    own_blocks = pltpu.make_async_copy(states_in.at[0, core, :, 0], blocks.at[core], own_sem.at[0])
    own_pack = pltpu.make_async_copy(pack_in, pack.at[core], own_sem.at[1])
    own_blocks.start()
    own_pack.start()
    for copy in env_copies:
        copy.start()

    barrier = pltpu.get_barrier_semaphore()
    pl.semaphore_signal(barrier, inc=1, device_id=(other, k), device_id_type=MESH)
    for step, sends, receives in peers_at:
        @pl.when(sends)
        def _():
            pl.semaphore_signal(barrier, inc=1, device_id=(core, k + step), device_id_type=MESH)

        @pl.when(receives)
        def _():
            pl.semaphore_signal(barrier, inc=1, device_id=(core, k - step), device_id_type=MESH)

    peers = 1
    for step, sends, receives in peers_at:
        peers = peers + sends.astype(jnp.int32) + receives.astype(jnp.int32)
    pl.semaphore_wait(barrier, peers)

    swaps = [
        pltpu.make_async_remote_copy(
            src_ref=source, dst_ref=target, send_sem=swap_send.at[i], recv_sem=swap_recv.at[i],
            device_id=(other, k), device_id_type=MESH,
        )
        for i, (source, target) in enumerate(
            [(pack_in, pack.at[core]), (states_in.at[0, other, :, 0], blocks.at[core])]
        )
    ]
    for swap in swaps:
        swap.start()

    proj[W] = jnp.zeros((BLK, 4 * BLK), BF)
    for slot in range(3):
        for c, (low, many) in enumerate(SPANS):
            @pl.when(jnp.logical_not(route(slot, c)[3]))
            def _():
                for site in range(2):
                    got[site, slot, low:low + many] = jnp.zeros((many, BLK, BLK), BF)

    def await_site(site):
        @pl.when(core == site)
        def _():
            own_blocks.wait()
            own_pack.wait()

        @pl.when(core != site)
        def _():
            for swap in swaps:
                swap.wait_recv()

    def prepare(site):
        spread = (lax.broadcasted_iota(jnp.int32, (W * SUB, SUB), 0) >> 4) == lax.broadcasted_iota(
            jnp.int32, (W * SUB, SUB), 1
        )
        spread = jnp.where(spread, 1.0, 0.0).astype(BF)
        widen = lax.broadcasted_iota(jnp.int32, (BLK, 256), 0) == (
            lax.broadcasted_iota(jnp.int32, (BLK, 256), 1) >> 4
        )
        widen = jnp.where(widen, 1.0, 0.0).astype(BF)
        same = (lax.broadcasted_iota(jnp.int32, (W * SUB, 256), 0) & 15) == (
            lax.broadcasted_iota(jnp.int32, (W * SUB, 256), 1) & 15
        )
        for s in range(4):
            tall = jnp.dot(spread, pack[site, s], preferred_element_type=F32).astype(BF)
            wide = jnp.dot(tall, widen, preferred_element_type=F32)
            kron[s] = jnp.where(same, wide, 0.0).astype(BF)
            block = blocks[site, s]
            joined[:, s * BLK:(s + 1) * BLK] = block
            turned[s] = block.astype(F32).T.astype(BF)

    def project(site, c):
        low, many = SPANS[c]
        rows = env[site, low:low + many].reshape(many * BLK, BLK)
        product = jnp.dot(rows, joined[...], preferred_element_type=F32).astype(BF)
        proj[low:low + many] = product.reshape(many, BLK, 4 * BLK)

    def part_copy(site, slot, c):
        state, step = route(slot, c)[:2]
        span = pl.ds(*SPANS[c])
        return pltpu.make_async_remote_copy(
            src_ref=parts.at[site, state, span], dst_ref=got.at[site, slot, span],
            send_sem=part_send.at[site, slot, c], recv_sem=part_recv.at[site, slot, c],
            device_id=(core, k + step), device_id_type=MESH,
        )

    def send(site, slot, c):
        @pl.when(route(slot, c)[2])
        def _():
            part_copy(site, slot, c).start()

    def receive(site, slot, c):
        @pl.when(route(slot, c)[3])
        def _():
            part_copy(site, slot, c).wait_recv()

    def pass_on(site, c):
        slot = 0 if c in RIGHT_FIRST else 1
        low, many = SPANS[c]
        receive(site, 2, c)
        for v in range(low, low + many):
            both = parts[site, slot + 1, v].astype(F32) + got[site, 2, v].astype(F32)
            parts[site, slot + 1, v] = both.astype(BF)
        send(site, slot, c)

    def mix_and_send(site, s):
        lanes = slice(s * BLK, (s + 1) * BLK)
        for i in range(BLK // (2 * SUB)):
            low, mid, high = 2 * i * SUB, (2 * i + 1) * SUB, (2 * i + 2) * SUB
            right = jnp.concatenate(
                [proj[:, low:mid, lanes].reshape(256, BLK), proj[:, mid:high, lanes].reshape(256, BLK)], axis=1
            )
            product = jnp.dot(kron[s], right, preferred_element_type=F32).astype(BF)
            for v in range(W):
                mixed[low:mid, v * BLK:(v + 1) * BLK] = product[v * SUB:(v + 1) * SUB, :BLK]
                mixed[mid:high, v * BLK:(v + 1) * BLK] = product[v * SUB:(v + 1) * SUB, BLK:]
        for c, (low, many) in enumerate(SPANS):
            product = jnp.dot(
                turned[s], mixed[:, low * BLK:(low + many) * BLK], preferred_element_type=F32
            ).astype(BF)
            for v in range(many):
                parts[site, s, low + v] = product[:, v * BLK:(v + 1) * BLK]
            if s == 3:
                send(site, 2, c)
            elif s == 2 and c in RIGHT_FIRST:
                send(site, 1, c)
            elif s == 1 and c not in RIGHT_FIRST:
                send(site, 0, c)

    def out_copies(site, c):
        span = pl.ds(*SPANS[c])
        source, target = env.at[site + 1, span], out.at[0, core, 0, span]
        local = pltpu.make_async_copy(source, target, out_sem.at[c])
        remote = pltpu.make_async_remote_copy(
            src_ref=source, dst_ref=target, send_sem=out_send.at[c], recv_sem=out_recv.at[c],
            device_id=(other, k), device_id_type=MESH,
        )
        return local, remote

    def combine(site, c):
        receive(site, 0, c)
        receive(site, 1, c)

        size = pack[site, 4].astype(F32)[0:1]
        live = (lax.broadcasted_iota(jnp.int32, (BLK, BLK), 0).astype(F32) < size) & (
            lax.broadcasted_iota(jnp.int32, (BLK, BLK), 1).astype(F32) < size
        )
        low, many = SPANS[c]
        for v in range(low, low + many):
            total = parts[site, 0, v].astype(F32) + got[site, 1, v].astype(F32)
            total = total + got[site, 0, v].astype(F32)
            env[site + 1, v] = jnp.where(live, total, 0.0).astype(BF)
        local, remote = out_copies(site, c)

        @pl.when(core == site)
        def _():
            local.start()

        @pl.when(core != site)
        def _():
            remote.start()

    order = (0, 2, 1, 3)
    for site in range(2):
        await_site(site)
        prepare(site)
        for c in order:
            if site == 0:
                env_copies[c].wait()
            else:
                combine(0, c)
            project(site, c)
        for s in (3, 2, 1, 0):
            mix_and_send(site, s)
        for c in order:
            pass_on(site, c)
    for c in order:
        combine(1, c)

    for swap in swaps:
        swap.wait_send()
    for site in range(2):
        for slot in range(3):
            for c in range(CHUNKS):
                @pl.when(route(slot, c)[2])
                def _():
                    part_copy(site, slot, c).wait_send()
    for site in range(2):
        for c in range(CHUNKS):
            local, remote = out_copies(site, c)

            @pl.when(core == site)
            def _():
                local.wait()
                remote.wait_recv()

            @pl.when(core != site)
            def _():
                remote.wait_send()


def on_device(env_first, states, mpo, block_rows, present):
    down_charge = lax.axis_index("sector") % QD
    inside = jnp.where(jnp.arange(4) >= 2, (down_charge < QD - 1).astype(F32), 1.0)
    keep = present[0, :, 0].astype(F32) * inside
    coupling = jnp.swapaxes(mpo[0], 1, 2).astype(F32) * keep[:, None, None]
    coupling = jnp.pad(coupling, ((0, 0), (0, SUB - W), (0, BLK - W)))
    size = jnp.broadcast_to(block_rows[0, 0].astype(F32), (1, SUB, BLK))
    pack = jnp.concatenate([coupling, size], axis=0).astype(BF)
    anywhere = pl.BlockSpec(memory_space=pl.ANY)
    return pl.pallas_call(
        kernel,
        out_shape=jax.ShapeDtypeStruct((1, 2, 1, W, BLK, BLK), BF),
        in_specs=[pl.BlockSpec(memory_space=pltpu.HBM)] * 2 + [anywhere],
        out_specs=anywhere,
        scratch_shapes=[
            pltpu.VMEM((3, W, BLK, BLK), BF),
            pltpu.VMEM((2, 4, BLK, BLK), BF),
            pltpu.VMEM((2, 5, SUB, BLK), BF),
            pltpu.VMEM((BLK, 4 * BLK), BF),
            pltpu.VMEM((4, BLK, BLK), BF),
            pltpu.VMEM((4, W * SUB, 256), BF),
            pltpu.VMEM((W + 1, BLK, 4 * BLK), BF),
            pltpu.VMEM((BLK, W * BLK), BF),
            pltpu.VMEM((2, 4, W, BLK, BLK), BF),
            pltpu.VMEM((2, 3, W, BLK, BLK), BF),
            pltpu.SemaphoreType.DMA((CHUNKS,)),
            pltpu.SemaphoreType.DMA((2,)),
            pltpu.SemaphoreType.DMA((2, 3, CHUNKS)),
            pltpu.SemaphoreType.DMA((2, 3, CHUNKS)),
            pltpu.SemaphoreType.DMA((2,)),
            pltpu.SemaphoreType.DMA((2,)),
            pltpu.SemaphoreType.DMA((CHUNKS,)),
            pltpu.SemaphoreType.DMA((CHUNKS,)),
            pltpu.SemaphoreType.DMA((CHUNKS,)),
        ],
        compiler_params=pltpu.CompilerParams(
            collective_id=0, has_side_effects=True, vmem_limit_bytes=67043328
        ),
    )(env_first, states, pack)


def solution(mesh):
    placed = (
        P(None, "sector", None, None, None),
        P("chain", None, None, "sector", None, None),
        P("chain", None, None, None),
        P("chain", "sector"),
        P("chain", None, "sector"),
    )
    return jax.shard_map(
        on_device,
        mesh=mesh,
        in_specs=placed,
        out_specs=P("chain", None, "sector", None, None, None),
        check_vma=False,
    )
```

```python
import jax
import jax.numpy as jnp
from jax import lax
from jax.experimental import pallas as pl
from jax.experimental.pallas import tpu as pltpu
from jax.sharding import PartitionSpec as P

QD = 4
W = 15
BLK = 128
SUB = 16
SPANS = ((0, 4), (4, 4), (8, 4), (12, 3))
CHUNKS = len(SPANS)
MESH = pl.DeviceIdType.MESH
BF = jnp.bfloat16
F32 = jnp.float32


def kernel(
    env_in, states_in, pack_in, out,
    env, near_env, blocks, near_blocks, pack, near_pack, joined, turned, kron, proj, mixed, parts, merged, got,
    env_sem, own_sem, swap_send, swap_recv, near_send, near_recv, env_send, env_recv, got_send, got_recv,
    out_sem, out_send, out_recv,
):
    sectors = lax.axis_size("sector")
    core, k = lax.axis_index("chain"), lax.axis_index("sector")
    other = 1 - core
    down = lax.rem(k, QD)
    right = (jnp.int32(1), down < QD - 1, down > 0)
    up = (jnp.int32(QD), k < sectors - QD, k >= QD)
    first = tuple(jnp.where(core == 0, r, u) for r, u in zip(right, up))
    second = tuple(jnp.where(core == 0, u, r) for r, u in zip(right, up))
    step, goes, comes = first
    step_after, goes_after, comes_after = second
    state_first = jnp.where(core == 0, 2, 1)
    state_after = 3 - state_first

    own_blocks = pltpu.make_async_copy(states_in.at[0, core, :, 0], blocks.at[core], own_sem.at[0])
    own_pack = pltpu.make_async_copy(pack_in, pack.at[core], own_sem.at[1])
    own_env = [
        pltpu.make_async_copy(env_in.at[core, 0, pl.ds(*SPANS[c])], env.at[0, pl.ds(*SPANS[c])], env_sem.at[c])
        for c in range(CHUNKS)
    ]
    own_blocks.start()
    own_pack.start()
    for copy in own_env:
        copy.start()

    barrier = pltpu.get_barrier_semaphore()

    def greet(condition, device):
        @pl.when(condition)
        def _():
            pl.semaphore_signal(barrier, inc=1, device_id=device, device_id_type=MESH)

    pl.semaphore_signal(barrier, inc=1, device_id=(other, k), device_id_type=MESH)
    greet(goes, (core, k + step))
    greet(comes, (core, k - step))
    greet(goes_after, (core, k + step_after))
    greet(comes_after, (core, k - step_after))
    greet(goes_after, (other, k + step_after))
    greet(comes, (other, k - step))
    pl.semaphore_wait(
        barrier,
        1 + 2 * goes_after.astype(jnp.int32) + 2 * comes.astype(jnp.int32)
        + goes.astype(jnp.int32) + comes_after.astype(jnp.int32),
    )

    def remote(source, target, send_sem, recv_sem, device):
        return pltpu.make_async_remote_copy(
            src_ref=source, dst_ref=target, send_sem=send_sem, recv_sem=recv_sem,
            device_id=device, device_id_type=MESH,
        )

    def when_do(condition, copies, action):
        @pl.when(condition)
        def _():
            for copy in copies:
                getattr(copy, action)()

    def near_copies(site, target, state, device, way):
        return [
            remote(source, sink, near_send.at[way, i], near_recv.at[site, i], device)
            for i, (source, sink) in enumerate([
                (pack_in, near_pack.at[site]),
                (states_in.at[0, target, 3, 0], near_blocks.at[site, 1]),
                (states_in.at[0, target, state, 0], near_blocks.at[site, 0]),
            ])
        ]

    def env_copy(site, c):
        span = pl.ds(*SPANS[c])
        source = env_in.at[core, 0, span] if site == 0 else env.at[1, span]
        return remote(
            source, near_env.at[site, span], env_send.at[site, c], env_recv.at[site, c], (core, k + step)
        )

    def got_copy(site, c):
        span = pl.ds(*SPANS[c])
        return remote(
            merged.at[site, span], got.at[site, span], got_send.at[site, c], got_recv.at[site, c],
            (core, k + step_after),
        )

    swaps = [
        remote(source, target, swap_send.at[i], swap_recv.at[i], (other, k))
        for i, (source, target) in enumerate(
            [(pack_in, pack.at[core]), (states_in.at[0, other, :, 0], blocks.at[core])]
        )
    ]
    near_same = near_copies(core, core, state_first, (core, k + step), 0)
    near_other = near_copies(core, other, state_after, (other, k + step_after), 1)
    for swap in swaps:
        swap.start()
    when_do(goes, near_same, "start")
    when_do(goes_after, near_other, "start")
    when_do(goes, [env_copy(0, c) for c in range(CHUNKS)], "start")

    proj[:, W] = jnp.zeros((2, BLK, 2 * BLK), BF)

    @pl.when(jnp.logical_not(comes))
    def _():
        near_blocks[...] = jnp.zeros_like(near_blocks)
        near_pack[...] = jnp.zeros_like(near_pack)
        near_env[...] = jnp.zeros_like(near_env)

    @pl.when(jnp.logical_not(comes_after))
    def _():
        got[...] = jnp.zeros_like(got)

    def prepare(q, coupling, block):
        spread = (lax.broadcasted_iota(jnp.int32, (W * SUB, SUB), 0) >> 4) == lax.broadcasted_iota(
            jnp.int32, (W * SUB, SUB), 1
        )
        spread = jnp.where(spread, 1.0, 0.0).astype(BF)
        widen = lax.broadcasted_iota(jnp.int32, (BLK, 256), 0) == (
            lax.broadcasted_iota(jnp.int32, (BLK, 256), 1) >> 4
        )
        widen = jnp.where(widen, 1.0, 0.0).astype(BF)
        same = (lax.broadcasted_iota(jnp.int32, (W * SUB, 256), 0) & 15) == (
            lax.broadcasted_iota(jnp.int32, (W * SUB, 256), 1) & 15
        )
        tall = jnp.dot(spread, coupling, preferred_element_type=F32).astype(BF)
        wide = jnp.dot(tall, widen, preferred_element_type=F32)
        kron[q] = jnp.where(same, wide, 0.0).astype(BF)
        joined[q // 2, :, (q % 2) * BLK:(q % 2 + 1) * BLK] = block
        turned[q] = block.astype(F32).T.astype(BF)

    def prepare_own(site):
        @pl.when(core == site)
        def _():
            own_blocks.wait()
            own_pack.wait()

        when_do(core != site, swaps, "wait_recv")
        prepare(0, pack[site, 0], blocks[site, 0])
        prepare(1, pack[site, state_after], blocks[site, state_after])

    def prepare_near(site):
        when_do(comes, near_copies(site, core, state_first, (core, k + step), 0), "wait_recv")
        prepare(2, near_pack[site, state_first], near_blocks[site, 0])
        prepare(3, near_pack[site, 3], near_blocks[site, 1])

    def project(half, source, c):
        low, many = SPANS[c]
        rows = source[low:low + many].reshape(many * BLK, BLK)
        product = jnp.dot(rows, joined[half], preferred_element_type=F32).astype(BF)
        proj[half, low:low + many] = product.reshape(many, BLK, 2 * BLK)

    def mix(site, q):
        half, lanes = q // 2, slice((q % 2) * BLK, (q % 2 + 1) * BLK)
        for i in range(BLK // (2 * SUB)):
            low, mid, high = 2 * i * SUB, (2 * i + 1) * SUB, (2 * i + 2) * SUB
            pair = jnp.concatenate(
                [proj[half, :, low:mid, lanes].reshape(256, BLK), proj[half, :, mid:high, lanes].reshape(256, BLK)],
                axis=1,
            )
            product = jnp.dot(kron[q], pair, preferred_element_type=F32).astype(BF)
            for v in range(W):
                mixed[low:mid, v * BLK:(v + 1) * BLK] = product[v * SUB:(v + 1) * SUB, :BLK]
                mixed[mid:high, v * BLK:(v + 1) * BLK] = product[v * SUB:(v + 1) * SUB, BLK:]
        for c, (low, many) in enumerate(SPANS):
            product = jnp.dot(
                turned[q], mixed[:, low * BLK:(low + many) * BLK], preferred_element_type=F32
            )
            for v in range(many):
                part = product[:, v * BLK:(v + 1) * BLK]
                if q == 3:
                    merged[site, low + v] = (part + parts[1, low + v].astype(F32)).astype(BF)
                else:
                    parts[q, low + v] = part.astype(BF)
            if q == 3:
                when_do(goes_after, [got_copy(site, c)], "start")

    def out_copies(site, c):
        span = pl.ds(*SPANS[c])
        source, target = env.at[site + 1, span], out.at[0, core, 0, span]
        local = pltpu.make_async_copy(source, target, out_sem.at[c])
        return local, remote(source, target, out_send.at[c], out_recv.at[c], (other, k))

    def combine(site, c):
        when_do(comes_after, [got_copy(site, c)], "wait_recv")
        size = pack[site, 4].astype(F32)[0:1]
        live = (lax.broadcasted_iota(jnp.int32, (BLK, BLK), 0).astype(F32) < size) & (
            lax.broadcasted_iota(jnp.int32, (BLK, BLK), 1).astype(F32) < size
        )
        low, many = SPANS[c]
        for v in range(low, low + many):
            total = parts[0, v].astype(F32) + parts[2, v].astype(F32) + got[site, v].astype(F32)
            env[site + 1, v] = jnp.where(live, total, 0.0).astype(BF)
        if site == 0:
            when_do(goes, [env_copy(1, c)], "start")
        local, across = out_copies(site, c)
        when_do(core == site, [local], "start")
        when_do(core != site, [across], "start")

    for site in range(2):
        prepare_own(site)
        if site == 1:
            prepare_near(site)
        for c in range(CHUNKS):
            if site == 0:
                own_env[c].wait()
            else:
                combine(0, c)
            project(0, env.at[site], c)
        mix(site, 1)
        mix(site, 0)
        if site == 0:
            prepare_near(site)
        for c in range(CHUNKS):
            when_do(comes, [env_copy(site, c)], "wait_recv")
            project(1, near_env.at[site], c)
        mix(site, 3)
        mix(site, 2)
    for c in range(CHUNKS):
        combine(1, c)

    for swap in swaps:
        swap.wait_send()
    when_do(goes, near_same, "wait_send")
    when_do(goes_after, near_other, "wait_send")
    for site in range(2):
        when_do(goes, [env_copy(site, c) for c in range(CHUNKS)], "wait_send")
        when_do(goes_after, [got_copy(site, c) for c in range(CHUNKS)], "wait_send")
    for site in range(2):
        for c in range(CHUNKS):
            local, across = out_copies(site, c)
            @pl.when(core == site)
            def _():
                local.wait()
                across.wait_recv()

            when_do(core != site, [across], "wait_send")


def on_device(env_first, states, mpo, block_rows, present):
    down_charge = lax.axis_index("sector") % QD
    inside = jnp.where(jnp.arange(4) >= 2, (down_charge < QD - 1).astype(F32), 1.0)
    keep = present[0, :, 0].astype(F32) * inside
    coupling = jnp.swapaxes(mpo[0], 1, 2).astype(F32) * keep[:, None, None]
    coupling = jnp.pad(coupling, ((0, 0), (0, SUB - W), (0, BLK - W)))
    size = jnp.broadcast_to(block_rows[0, 0].astype(F32), (1, SUB, BLK))
    pack = jnp.concatenate([coupling, size], axis=0).astype(BF)
    anywhere = pl.BlockSpec(memory_space=pl.ANY)
    return pl.pallas_call(
        kernel,
        out_shape=jax.ShapeDtypeStruct((1, 2, 1, W, BLK, BLK), BF),
        in_specs=[pl.BlockSpec(memory_space=pltpu.HBM)] * 2 + [anywhere],
        out_specs=anywhere,
        scratch_shapes=[
            pltpu.VMEM((3, W, BLK, BLK), BF),
            pltpu.VMEM((2, W, BLK, BLK), BF),
            pltpu.VMEM((2, 4, BLK, BLK), BF),
            pltpu.VMEM((2, 2, BLK, BLK), BF),
            pltpu.VMEM((2, 5, SUB, BLK), BF),
            pltpu.VMEM((2, 5, SUB, BLK), BF),
            pltpu.VMEM((2, BLK, 2 * BLK), BF),
            pltpu.VMEM((4, BLK, BLK), BF),
            pltpu.VMEM((4, W * SUB, 256), BF),
            pltpu.VMEM((2, W + 1, BLK, 2 * BLK), BF),
            pltpu.VMEM((BLK, W * BLK), BF),
            pltpu.VMEM((3, W, BLK, BLK), BF),
            pltpu.VMEM((2, W, BLK, BLK), BF),
            pltpu.VMEM((2, W, BLK, BLK), BF),
            pltpu.SemaphoreType.DMA((CHUNKS,)),
            pltpu.SemaphoreType.DMA((2,)),
            pltpu.SemaphoreType.DMA((2,)),
            pltpu.SemaphoreType.DMA((2,)),
            pltpu.SemaphoreType.DMA((2, 3)),
            pltpu.SemaphoreType.DMA((2, 3)),
            pltpu.SemaphoreType.DMA((2, CHUNKS)),
            pltpu.SemaphoreType.DMA((2, CHUNKS)),
            pltpu.SemaphoreType.DMA((2, CHUNKS)),
            pltpu.SemaphoreType.DMA((2, CHUNKS)),
            pltpu.SemaphoreType.DMA((CHUNKS,)),
            pltpu.SemaphoreType.DMA((CHUNKS,)),
            pltpu.SemaphoreType.DMA((CHUNKS,)),
        ],
        compiler_params=pltpu.CompilerParams(
            collective_id=0, has_side_effects=True, vmem_limit_bytes=67043328
        ),
    )(env_first, states, pack)


def solution(mesh):
    placed = (
        P(None, "sector", None, None, None),
        P("chain", None, None, "sector", None, None),
        P("chain", None, None, None),
        P("chain", "sector"),
        P("chain", None, "sector"),
    )
    return jax.shard_map(
        on_device,
        mesh=mesh,
        in_specs=placed,
        out_specs=P("chain", None, "sector", None, None, None),
        check_vma=False,
    )
```

```python
import jax
import jax.numpy as jnp
from jax import lax
from jax.experimental import pallas as pl
from jax.experimental.pallas import tpu as pltpu
from jax.sharding import PartitionSpec as P

QD = 4
W = 15
BLK = 128
SUB = 16
SPANS = ((0, 4), (4, 4), (8, 4), (12, 3))
CHUNKS = len(SPANS)
MESH = pl.DeviceIdType.MESH
BF = jnp.bfloat16
F32 = jnp.float32


def kernel(
    env_in, states_in, pack_in, out,
    env, near_env, blocks, near_blocks, pack, near_pack, joined, turned, kron, proj, mixed, parts, merged, got,
    env_sem, own_sem, swap_send, swap_recv, near_send, near_recv, env_send, env_recv, got_send, got_recv,
    out_sem, out_send, out_recv,
):
    sectors = lax.axis_size("sector")
    core, k = lax.axis_index("chain"), lax.axis_index("sector")
    other = 1 - core
    down = lax.rem(k, QD)
    right = (jnp.int32(1), down < QD - 1, down > 0)
    up = (jnp.int32(QD), k < sectors - QD, k >= QD)
    first = tuple(jnp.where(core == 0, r, u) for r, u in zip(right, up))
    second = tuple(jnp.where(core == 0, u, r) for r, u in zip(right, up))
    step, goes, comes = first
    step_after, goes_after, comes_after = second
    state_first = jnp.where(core == 0, 2, 1)
    state_after = 3 - state_first

    own_blocks = pltpu.make_async_copy(states_in.at[0, core, :, 0], blocks.at[core], own_sem.at[0])
    own_pack = pltpu.make_async_copy(pack_in, pack.at[core], own_sem.at[1])
    own_env = [
        pltpu.make_async_copy(env_in.at[core, 0, pl.ds(*SPANS[c])], env.at[0, pl.ds(*SPANS[c])], env_sem.at[c])
        for c in range(CHUNKS)
    ]
    own_blocks.start()
    own_pack.start()
    for copy in own_env:
        copy.start()

    barrier = pltpu.get_barrier_semaphore()

    def greet(condition, device):
        @pl.when(condition)
        def _():
            pl.semaphore_signal(barrier, inc=1, device_id=device, device_id_type=MESH)

    pl.semaphore_signal(barrier, inc=1, device_id=(other, k), device_id_type=MESH)
    greet(goes, (core, k + step))
    greet(comes, (core, k - step))
    greet(goes_after, (core, k + step_after))
    greet(comes_after, (core, k - step_after))
    greet(goes_after, (other, k + step_after))
    greet(comes, (other, k - step))
    pl.semaphore_wait(
        barrier,
        1 + 2 * goes_after.astype(jnp.int32) + 2 * comes.astype(jnp.int32)
        + goes.astype(jnp.int32) + comes_after.astype(jnp.int32),
    )

    def remote(source, target, send_sem, recv_sem, device):
        return pltpu.make_async_remote_copy(
            src_ref=source, dst_ref=target, send_sem=send_sem, recv_sem=recv_sem,
            device_id=device, device_id_type=MESH,
        )

    def when_do(condition, copies, action):
        @pl.when(condition)
        def _():
            for copy in copies:
                getattr(copy, action)()

    def near_copies(site, target, state, device, way):
        return [
            remote(source, sink, near_send.at[way, i], near_recv.at[site, i], device)
            for i, (source, sink) in enumerate([
                (pack_in, near_pack.at[site]),
                (states_in.at[0, target, 3, 0], near_blocks.at[site, 1]),
                (states_in.at[0, target, state, 0], near_blocks.at[site, 0]),
            ])
        ]

    def env_copy(site, c):
        span = pl.ds(*SPANS[c])
        source = env_in.at[core, 0, span] if site == 0 else env.at[1, span]
        return remote(
            source, near_env.at[site, span], env_send.at[site, c], env_recv.at[site, c], (core, k + step)
        )

    def got_copy(site, c):
        span = pl.ds(*SPANS[c])
        return remote(
            merged.at[site, span], got.at[site, span], got_send.at[site, c], got_recv.at[site, c],
            (core, k + step_after),
        )

    swaps = [
        remote(source, target, swap_send.at[i], swap_recv.at[i], (other, k))
        for i, (source, target) in enumerate(
            [(pack_in, pack.at[core]), (states_in.at[0, other, :, 0], blocks.at[core])]
        )
    ]
    near_same = near_copies(core, core, state_first, (core, k + step), 0)
    near_other = near_copies(core, other, state_after, (other, k + step_after), 1)
    for swap in swaps:
        swap.start()
    when_do(goes & (core == 0), near_same, "start")
    when_do(goes_after & (core == 0), near_other, "start")
    when_do(goes, [env_copy(0, c) for c in range(CHUNKS)], "start")
    when_do(goes & (core == 1), near_same, "start")
    when_do(goes_after & (core == 1), near_other, "start")

    proj[:, W] = jnp.zeros((2, BLK, 2 * BLK), BF)

    @pl.when(jnp.logical_not(comes))
    def _():
        near_blocks[...] = jnp.zeros_like(near_blocks)
        near_pack[...] = jnp.zeros_like(near_pack)
        near_env[...] = jnp.zeros_like(near_env)

    @pl.when(jnp.logical_not(comes_after))
    def _():
        got[...] = jnp.zeros_like(got)

    def prepare(q, coupling, block):
        spread = (lax.broadcasted_iota(jnp.int32, (W * SUB, SUB), 0) >> 4) == lax.broadcasted_iota(
            jnp.int32, (W * SUB, SUB), 1
        )
        spread = jnp.where(spread, 1.0, 0.0).astype(BF)
        widen = lax.broadcasted_iota(jnp.int32, (BLK, 256), 0) == (
            lax.broadcasted_iota(jnp.int32, (BLK, 256), 1) >> 4
        )
        widen = jnp.where(widen, 1.0, 0.0).astype(BF)
        same = (lax.broadcasted_iota(jnp.int32, (W * SUB, 256), 0) & 15) == (
            lax.broadcasted_iota(jnp.int32, (W * SUB, 256), 1) & 15
        )
        tall = jnp.dot(spread, coupling, preferred_element_type=F32).astype(BF)
        wide = jnp.dot(tall, widen, preferred_element_type=F32)
        kron[q] = jnp.where(same, wide, 0.0).astype(BF)
        joined[q // 2, :, (q % 2) * BLK:(q % 2 + 1) * BLK] = block
        turned[q] = block.astype(F32).T.astype(BF)

    def prepare_own(site):
        @pl.when(core == site)
        def _():
            own_blocks.wait()
            own_pack.wait()

        when_do(core != site, swaps, "wait_recv")
        prepare(0, pack[site, 0], blocks[site, 0])
        prepare(1, pack[site, state_after], blocks[site, state_after])

    def prepare_near(site):
        when_do(comes, near_copies(site, core, state_first, (core, k + step), 0), "wait_recv")
        prepare(2, near_pack[site, state_first], near_blocks[site, 0])
        prepare(3, near_pack[site, 3], near_blocks[site, 1])

    def project(half, source, c):
        low, many = SPANS[c]
        rows = source[low:low + many].reshape(many * BLK, BLK)
        product = jnp.dot(rows, joined[half], preferred_element_type=F32).astype(BF)
        proj[half, low:low + many] = product.reshape(many, BLK, 2 * BLK)

    def mix(site, q):
        half, lanes = q // 2, slice((q % 2) * BLK, (q % 2 + 1) * BLK)
        for i in range(BLK // (2 * SUB)):
            low, mid, high = 2 * i * SUB, (2 * i + 1) * SUB, (2 * i + 2) * SUB
            pair = jnp.concatenate(
                [proj[half, :, low:mid, lanes].reshape(256, BLK), proj[half, :, mid:high, lanes].reshape(256, BLK)],
                axis=1,
            )
            product = jnp.dot(kron[q], pair, preferred_element_type=F32).astype(BF)
            for v in range(W):
                mixed[low:mid, v * BLK:(v + 1) * BLK] = product[v * SUB:(v + 1) * SUB, :BLK]
                mixed[mid:high, v * BLK:(v + 1) * BLK] = product[v * SUB:(v + 1) * SUB, BLK:]
        for c, (low, many) in enumerate(SPANS):
            product = jnp.dot(
                turned[q], mixed[:, low * BLK:(low + many) * BLK], preferred_element_type=F32
            )
            for v in range(many):
                part = product[:, v * BLK:(v + 1) * BLK]
                if q == 3:
                    merged[site, low + v] = (part + parts[1, low + v].astype(F32)).astype(BF)
                else:
                    parts[q, low + v] = part.astype(BF)
            if q == 3:
                when_do(goes_after, [got_copy(site, c)], "start")

    def out_copies(site, c):
        span = pl.ds(*SPANS[c])
        source, target = env.at[site + 1, span], out.at[0, core, 0, span]
        local = pltpu.make_async_copy(source, target, out_sem.at[c])
        return local, remote(source, target, out_send.at[c], out_recv.at[c], (other, k))

    def combine(site, c):
        when_do(comes_after, [got_copy(site, c)], "wait_recv")
        size = pack[site, 4].astype(F32)[0:1]
        live = (lax.broadcasted_iota(jnp.int32, (BLK, BLK), 0).astype(F32) < size) & (
            lax.broadcasted_iota(jnp.int32, (BLK, BLK), 1).astype(F32) < size
        )
        low, many = SPANS[c]
        for v in range(low, low + many):
            total = parts[0, v].astype(F32) + parts[2, v].astype(F32) + got[site, v].astype(F32)
            env[site + 1, v] = jnp.where(live, total, 0.0).astype(BF)
        if site == 0:
            when_do(goes, [env_copy(1, c)], "start")
        local, across = out_copies(site, c)
        when_do(core == site, [local], "start")
        when_do(core != site, [across], "start")

    for site in range(2):
        prepare_own(site)
        if site == 1:
            prepare_near(site)
        for c in range(CHUNKS):
            if site == 0:
                own_env[c].wait()
            else:
                combine(0, c)
            project(0, env.at[site], c)
        mix(site, 1)
        mix(site, 0)
        if site == 0:
            prepare_near(site)
        for c in range(CHUNKS):
            when_do(comes, [env_copy(site, c)], "wait_recv")
            project(1, near_env.at[site], c)
        mix(site, 3)
        mix(site, 2)
    for c in range(CHUNKS):
        combine(1, c)

    for swap in swaps:
        swap.wait_send()
    when_do(goes, near_same, "wait_send")
    when_do(goes_after, near_other, "wait_send")
    for site in range(2):
        when_do(goes, [env_copy(site, c) for c in range(CHUNKS)], "wait_send")
        when_do(goes_after, [got_copy(site, c) for c in range(CHUNKS)], "wait_send")
    for site in range(2):
        for c in range(CHUNKS):
            local, across = out_copies(site, c)
            @pl.when(core == site)
            def _():
                local.wait()
                across.wait_recv()

            when_do(core != site, [across], "wait_send")


def on_device(env_first, states, mpo, block_rows, present):
    down_charge = lax.axis_index("sector") % QD
    inside = jnp.where(jnp.arange(4) >= 2, (down_charge < QD - 1).astype(F32), 1.0)
    keep = present[0, :, 0].astype(F32) * inside
    coupling = jnp.swapaxes(mpo[0], 1, 2).astype(F32) * keep[:, None, None]
    coupling = jnp.pad(coupling, ((0, 0), (0, SUB - W), (0, BLK - W)))
    size = jnp.broadcast_to(block_rows[0, 0].astype(F32), (1, SUB, BLK))
    pack = jnp.concatenate([coupling, size], axis=0).astype(BF)
    anywhere = pl.BlockSpec(memory_space=pl.ANY)
    return pl.pallas_call(
        kernel,
        out_shape=jax.ShapeDtypeStruct((1, 2, 1, W, BLK, BLK), BF),
        in_specs=[pl.BlockSpec(memory_space=pltpu.HBM)] * 2 + [anywhere],
        out_specs=anywhere,
        scratch_shapes=[
            pltpu.VMEM((3, W, BLK, BLK), BF),
            pltpu.VMEM((2, W, BLK, BLK), BF),
            pltpu.VMEM((2, 4, BLK, BLK), BF),
            pltpu.VMEM((2, 2, BLK, BLK), BF),
            pltpu.VMEM((2, 5, SUB, BLK), BF),
            pltpu.VMEM((2, 5, SUB, BLK), BF),
            pltpu.VMEM((2, BLK, 2 * BLK), BF),
            pltpu.VMEM((4, BLK, BLK), BF),
            pltpu.VMEM((4, W * SUB, 256), BF),
            pltpu.VMEM((2, W + 1, BLK, 2 * BLK), BF),
            pltpu.VMEM((BLK, W * BLK), BF),
            pltpu.VMEM((3, W, BLK, BLK), BF),
            pltpu.VMEM((2, W, BLK, BLK), BF),
            pltpu.VMEM((2, W, BLK, BLK), BF),
            pltpu.SemaphoreType.DMA((CHUNKS,)),
            pltpu.SemaphoreType.DMA((2,)),
            pltpu.SemaphoreType.DMA((2,)),
            pltpu.SemaphoreType.DMA((2,)),
            pltpu.SemaphoreType.DMA((2, 3)),
            pltpu.SemaphoreType.DMA((2, 3)),
            pltpu.SemaphoreType.DMA((2, CHUNKS)),
            pltpu.SemaphoreType.DMA((2, CHUNKS)),
            pltpu.SemaphoreType.DMA((2, CHUNKS)),
            pltpu.SemaphoreType.DMA((2, CHUNKS)),
            pltpu.SemaphoreType.DMA((CHUNKS,)),
            pltpu.SemaphoreType.DMA((CHUNKS,)),
            pltpu.SemaphoreType.DMA((CHUNKS,)),
        ],
        compiler_params=pltpu.CompilerParams(
            collective_id=0, has_side_effects=True, vmem_limit_bytes=48 * 1024 * 1024
        ),
    )(
        pltpu.with_memory_space_constraint(env_first, pltpu.HBM),
        pltpu.with_memory_space_constraint(states, pltpu.HBM),
        pack,
    )


def solution(mesh):
    placed = (
        P(None, "sector", None, None, None),
        P("chain", None, None, "sector", None, None),
        P("chain", None, None, None),
        P("chain", "sector"),
        P("chain", None, "sector"),
    )
    return jax.shard_map(
        on_device,
        mesh=mesh,
        in_specs=placed,
        out_specs=P("chain", None, "sector", None, None, None),
        check_vma=False,
    )
```

```python
import jax
import jax.numpy as jnp
from jax import lax
from jax.experimental import pallas as pl
from jax.experimental.pallas import tpu as pltpu
from jax.sharding import PartitionSpec as P

QD = 4
W = 15
BLK = 128
SUB = 16
SPANS = ((0, 4), (4, 4), (8, 4), (12, 2), (14, 1))
CHUNKS = len(SPANS)
MESH = pl.DeviceIdType.MESH
BF = jnp.bfloat16
F32 = jnp.float32


def kernel(
    env_in, states_in, pack_in, out,
    env, near_env, blocks, near_blocks, pack, near_pack, joined, turned, kron, proj, mixed, parts, merged, got,
    env_sem, own_sem, swap_send, swap_recv, near_send, near_recv, env_send, env_recv, got_send, got_recv,
    out_sem, out_send, out_recv,
):
    sectors = lax.axis_size("sector")
    core, k = lax.axis_index("chain"), lax.axis_index("sector")
    other = 1 - core
    down = lax.rem(k, QD)
    right = (jnp.int32(1), down < QD - 1, down > 0)
    up = (jnp.int32(QD), k < sectors - QD, k >= QD)
    first = tuple(jnp.where(core == 0, r, u) for r, u in zip(right, up))
    second = tuple(jnp.where(core == 0, u, r) for r, u in zip(right, up))
    step, goes, comes = first
    step_after, goes_after, comes_after = second
    state_first = jnp.where(core == 0, 2, 1)
    state_after = 3 - state_first

    own_blocks = pltpu.make_async_copy(states_in.at[0, core, :, 0], blocks.at[core], own_sem.at[0])
    own_pack = pltpu.make_async_copy(pack_in, pack.at[core], own_sem.at[1])
    own_env = [
        pltpu.make_async_copy(env_in.at[core, 0, pl.ds(*SPANS[c])], env.at[0, pl.ds(*SPANS[c])], env_sem.at[c])
        for c in range(CHUNKS)
    ]
    own_blocks.start()
    own_pack.start()
    for copy in own_env:
        copy.start()

    barrier = pltpu.get_barrier_semaphore()

    def greet(condition, device):
        @pl.when(condition)
        def _():
            pl.semaphore_signal(barrier, inc=1, device_id=device, device_id_type=MESH)

    pl.semaphore_signal(barrier, inc=1, device_id=(other, k), device_id_type=MESH)
    greet(goes, (core, k + step))
    greet(comes, (core, k - step))
    greet(goes_after, (core, k + step_after))
    greet(comes_after, (core, k - step_after))
    greet(goes_after, (other, k + step_after))
    greet(comes, (other, k - step))
    pl.semaphore_wait(
        barrier,
        1 + 2 * goes_after.astype(jnp.int32) + 2 * comes.astype(jnp.int32)
        + goes.astype(jnp.int32) + comes_after.astype(jnp.int32),
    )

    def remote(source, target, send_sem, recv_sem, device):
        return pltpu.make_async_remote_copy(
            src_ref=source, dst_ref=target, send_sem=send_sem, recv_sem=recv_sem,
            device_id=device, device_id_type=MESH,
        )

    def when_do(condition, copies, action):
        @pl.when(condition)
        def _():
            for copy in copies:
                getattr(copy, action)()

    def near_copies(site, target, state, device, way):
        return [
            remote(source, sink, near_send.at[way, i], near_recv.at[site, i], device)
            for i, (source, sink) in enumerate([
                (pack_in, near_pack.at[site]),
                (states_in.at[0, target, 3, 0], near_blocks.at[site, 1]),
                (states_in.at[0, target, state, 0], near_blocks.at[site, 0]),
            ])
        ]

    def env_copy(site, c):
        span = pl.ds(*SPANS[c])
        source = env_in.at[core, 0, span] if site == 0 else env.at[1, span]
        return remote(
            source, near_env.at[site, span], env_send.at[site, c], env_recv.at[site, c], (core, k + step)
        )

    def got_copy(site, c):
        span = pl.ds(*SPANS[c])
        return remote(
            merged.at[site, span], got.at[site, span], got_send.at[site, c], got_recv.at[site, c],
            (core, k + step_after),
        )

    swaps = [
        remote(source, target, swap_send.at[i], swap_recv.at[i], (other, k))
        for i, (source, target) in enumerate(
            [(pack_in, pack.at[core]), (states_in.at[0, other, :, 0], blocks.at[core])]
        )
    ]
    near_same = near_copies(core, core, state_first, (core, k + step), 0)
    near_other = near_copies(core, other, state_after, (other, k + step_after), 1)
    for swap in swaps:
        swap.start()
    when_do(goes & (core == 0), near_same, "start")
    when_do(goes_after & (core == 0), near_other, "start")
    when_do(goes, [env_copy(0, c) for c in range(CHUNKS)], "start")
    when_do(goes & (core == 1), near_same, "start")
    when_do(goes_after & (core == 1), near_other, "start")

    proj[:, W] = jnp.zeros((2, BLK, 2 * BLK), BF)

    @pl.when(jnp.logical_not(comes))
    def _():
        near_blocks[...] = jnp.zeros_like(near_blocks)
        near_pack[...] = jnp.zeros_like(near_pack)
        near_env[...] = jnp.zeros_like(near_env)

    @pl.when(jnp.logical_not(comes_after))
    def _():
        got[...] = jnp.zeros_like(got)

    def prepare(q, coupling, block):
        spread = (lax.broadcasted_iota(jnp.int32, (W * SUB, SUB), 0) >> 4) == lax.broadcasted_iota(
            jnp.int32, (W * SUB, SUB), 1
        )
        spread = jnp.where(spread, 1.0, 0.0).astype(BF)
        widen = lax.broadcasted_iota(jnp.int32, (BLK, 256), 0) == (
            lax.broadcasted_iota(jnp.int32, (BLK, 256), 1) >> 4
        )
        widen = jnp.where(widen, 1.0, 0.0).astype(BF)
        same = (lax.broadcasted_iota(jnp.int32, (W * SUB, 256), 0) & 15) == (
            lax.broadcasted_iota(jnp.int32, (W * SUB, 256), 1) & 15
        )
        tall = jnp.dot(spread, coupling, preferred_element_type=F32).astype(BF)
        wide = jnp.dot(tall, widen, preferred_element_type=F32)
        kron[q] = jnp.where(same, wide, 0.0).astype(BF)
        joined[q // 2, :, (q % 2) * BLK:(q % 2 + 1) * BLK] = block
        turned[q] = block.astype(F32).T.astype(BF)

    def prepare_own(site):
        @pl.when(core == site)
        def _():
            own_blocks.wait()
            own_pack.wait()

        when_do(core != site, swaps, "wait_recv")
        prepare(0, pack[site, 0], blocks[site, 0])
        prepare(1, pack[site, state_after], blocks[site, state_after])

    def prepare_near(site):
        when_do(comes, near_copies(site, core, state_first, (core, k + step), 0), "wait_recv")
        prepare(2, near_pack[site, state_first], near_blocks[site, 0])
        prepare(3, near_pack[site, 3], near_blocks[site, 1])

    def project(half, source, c):
        low, many = SPANS[c]
        rows = source[low:low + many].reshape(many * BLK, BLK)
        product = jnp.dot(rows, joined[half], preferred_element_type=F32).astype(BF)
        proj[half, low:low + many] = product.reshape(many, BLK, 2 * BLK)

    def mix(site, q):
        half, lanes = q // 2, slice((q % 2) * BLK, (q % 2 + 1) * BLK)
        for i in range(BLK // (2 * SUB)):
            low, mid, high = 2 * i * SUB, (2 * i + 1) * SUB, (2 * i + 2) * SUB
            pair = jnp.concatenate(
                [proj[half, :, low:mid, lanes].reshape(256, BLK), proj[half, :, mid:high, lanes].reshape(256, BLK)],
                axis=1,
            )
            product = jnp.dot(kron[q], pair, preferred_element_type=F32).astype(BF)
            for v in range(W):
                mixed[low:mid, v * BLK:(v + 1) * BLK] = product[v * SUB:(v + 1) * SUB, :BLK]
                mixed[mid:high, v * BLK:(v + 1) * BLK] = product[v * SUB:(v + 1) * SUB, BLK:]
        for c, (low, many) in enumerate(SPANS):
            product = jnp.dot(
                turned[q], mixed[:, low * BLK:(low + many) * BLK], preferred_element_type=F32
            )
            for v in range(many):
                part = product[:, v * BLK:(v + 1) * BLK]
                if q == 3:
                    merged[site, low + v] = (part + parts[1, low + v].astype(F32)).astype(BF)
                else:
                    parts[q, low + v] = part.astype(BF)
            if q == 3:
                when_do(goes_after, [got_copy(site, c)], "start")

    def out_copies(site, c):
        span = pl.ds(*SPANS[c])
        source, target = env.at[site + 1, span], out.at[0, core, 0, span]
        local = pltpu.make_async_copy(source, target, out_sem.at[c])
        return local, remote(source, target, out_send.at[c], out_recv.at[c], (other, k))

    def combine(site, c):
        when_do(comes_after, [got_copy(site, c)], "wait_recv")
        size = pack[site, 4].astype(F32)[0:1]
        live = (lax.broadcasted_iota(jnp.int32, (BLK, BLK), 0).astype(F32) < size) & (
            lax.broadcasted_iota(jnp.int32, (BLK, BLK), 1).astype(F32) < size
        )
        low, many = SPANS[c]
        for v in range(low, low + many):
            total = parts[0, v].astype(F32) + parts[2, v].astype(F32) + got[site, v].astype(F32)
            env[site + 1, v] = jnp.where(live, total, 0.0).astype(BF)
        if site == 0:
            when_do(goes, [env_copy(1, c)], "start")
        local, across = out_copies(site, c)
        when_do(core == site, [local], "start")
        when_do(core != site, [across], "start")

    for site in range(2):
        prepare_own(site)
        if site == 1:
            prepare_near(site)
        for c in range(CHUNKS):
            if site == 0:
                own_env[c].wait()
            else:
                combine(0, c)
            project(0, env.at[site], c)
        mix(site, 1)
        mix(site, 0)
        if site == 0:
            prepare_near(site)
        for c in range(CHUNKS):
            when_do(comes, [env_copy(site, c)], "wait_recv")
            project(1, near_env.at[site], c)
        mix(site, 3)
        mix(site, 2)
    for c in range(CHUNKS):
        combine(1, c)

    for swap in swaps:
        swap.wait_send()
    when_do(goes, near_same, "wait_send")
    when_do(goes_after, near_other, "wait_send")
    for site in range(2):
        when_do(goes, [env_copy(site, c) for c in range(CHUNKS)], "wait_send")
        when_do(goes_after, [got_copy(site, c) for c in range(CHUNKS)], "wait_send")
    for site in range(2):
        for c in range(CHUNKS):
            local, across = out_copies(site, c)
            @pl.when(core == site)
            def _():
                local.wait()
                across.wait_recv()

            when_do(core != site, [across], "wait_send")


def on_device(env_first, states, mpo, block_rows, present):
    down_charge = lax.axis_index("sector") % QD
    inside = jnp.where(jnp.arange(4) >= 2, (down_charge < QD - 1).astype(F32), 1.0)
    keep = present[0, :, 0].astype(F32) * inside
    coupling = jnp.swapaxes(mpo[0], 1, 2).astype(F32) * keep[:, None, None]
    coupling = jnp.pad(coupling, ((0, 0), (0, SUB - W), (0, BLK - W)))
    size = jnp.broadcast_to(block_rows[0, 0].astype(F32), (1, SUB, BLK))
    pack = jnp.concatenate([coupling, size], axis=0).astype(BF)
    anywhere = pl.BlockSpec(memory_space=pl.ANY)
    return pl.pallas_call(
        kernel,
        out_shape=jax.ShapeDtypeStruct((1, 2, 1, W, BLK, BLK), BF),
        in_specs=[pl.BlockSpec(memory_space=pltpu.HBM)] * 2 + [anywhere],
        out_specs=anywhere,
        scratch_shapes=[
            pltpu.VMEM((3, W, BLK, BLK), BF),
            pltpu.VMEM((2, W, BLK, BLK), BF),
            pltpu.VMEM((2, 4, BLK, BLK), BF),
            pltpu.VMEM((2, 2, BLK, BLK), BF),
            pltpu.VMEM((2, 5, SUB, BLK), BF),
            pltpu.VMEM((2, 5, SUB, BLK), BF),
            pltpu.VMEM((2, BLK, 2 * BLK), BF),
            pltpu.VMEM((4, BLK, BLK), BF),
            pltpu.VMEM((4, W * SUB, 256), BF),
            pltpu.VMEM((2, W + 1, BLK, 2 * BLK), BF),
            pltpu.VMEM((BLK, W * BLK), BF),
            pltpu.VMEM((3, W, BLK, BLK), BF),
            pltpu.VMEM((2, W, BLK, BLK), BF),
            pltpu.VMEM((2, W, BLK, BLK), BF),
            pltpu.SemaphoreType.DMA((CHUNKS,)),
            pltpu.SemaphoreType.DMA((2,)),
            pltpu.SemaphoreType.DMA((2,)),
            pltpu.SemaphoreType.DMA((2,)),
            pltpu.SemaphoreType.DMA((2, 3)),
            pltpu.SemaphoreType.DMA((2, 3)),
            pltpu.SemaphoreType.DMA((2, CHUNKS)),
            pltpu.SemaphoreType.DMA((2, CHUNKS)),
            pltpu.SemaphoreType.DMA((2, CHUNKS)),
            pltpu.SemaphoreType.DMA((2, CHUNKS)),
            pltpu.SemaphoreType.DMA((CHUNKS,)),
            pltpu.SemaphoreType.DMA((CHUNKS,)),
            pltpu.SemaphoreType.DMA((CHUNKS,)),
        ],
        compiler_params=pltpu.CompilerParams(
            collective_id=0, has_side_effects=True, vmem_limit_bytes=48 * 1024 * 1024
        ),
    )(
        pltpu.with_memory_space_constraint(env_first, pltpu.HBM),
        pltpu.with_memory_space_constraint(states, pltpu.HBM),
        pack,
    )


def solution(mesh):
    placed = (
        P(None, "sector", None, None, None),
        P("chain", None, None, "sector", None, None),
        P("chain", None, None, None),
        P("chain", "sector"),
        P("chain", None, "sector"),
    )
    return jax.shard_map(
        on_device,
        mesh=mesh,
        in_specs=placed,
        out_specs=P("chain", None, "sector", None, None, None),
        check_vma=False,
    )
```

```python
import jax
import jax.numpy as jnp
from jax import lax
from jax.experimental import pallas as pl
from jax.experimental.pallas import tpu as pltpu
from jax.sharding import PartitionSpec as P

QD = 4
W = 15
BLK = 128
SUB = 16
SPANS = ((0, 4), (4, 4), (8, 4), (12, 2), (14, 1))
CHUNKS = len(SPANS)
MESH = pl.DeviceIdType.MESH
BF = jnp.bfloat16
F32 = jnp.float32


def kernel(
    env_in, states_in, pack_in, out,
    env, near_env, blocks, near_blocks, pack, near_pack, joined, turned, kron, proj, mixed, parts, merged, got,
    env_sem, own_sem, swap_send, swap_recv, near_send, near_recv, env_send, env_recv, got_send, got_recv,
    out_sem, out_send, out_recv,
):
    sectors = lax.axis_size("sector")
    core, k = lax.axis_index("chain"), lax.axis_index("sector")
    other = 1 - core
    down = lax.rem(k, QD)
    right = (jnp.int32(1), down < QD - 1, down > 0)
    up = (jnp.int32(QD), k < sectors - QD, k >= QD)
    first = tuple(jnp.where(core == 0, r, u) for r, u in zip(right, up))
    second = tuple(jnp.where(core == 0, u, r) for r, u in zip(right, up))
    step, goes, comes = first
    step_after, goes_after, comes_after = second
    state_first = jnp.where(core == 0, 2, 1)
    state_after = 3 - state_first

    own_blocks = pltpu.make_async_copy(states_in.at[0, core, :, 0], blocks.at[core], own_sem.at[0])
    own_pack = pltpu.make_async_copy(pack_in, pack.at[core], own_sem.at[1])
    own_env = [
        pltpu.make_async_copy(env_in.at[core, 0, pl.ds(*SPANS[c])], env.at[0, pl.ds(*SPANS[c])], env_sem.at[c])
        for c in range(CHUNKS)
    ]
    own_blocks.start()
    own_pack.start()
    for copy in own_env:
        copy.start()

    barrier = pltpu.get_barrier_semaphore()

    def greet(condition, device):
        @pl.when(condition)
        def _():
            pl.semaphore_signal(barrier, inc=1, device_id=device, device_id_type=MESH)

    pl.semaphore_signal(barrier, inc=1, device_id=(other, k), device_id_type=MESH)
    greet(goes, (core, k + step))
    greet(comes, (core, k - step))
    greet(goes_after, (core, k + step_after))
    greet(comes_after, (core, k - step_after))
    greet(goes_after, (other, k + step_after))
    greet(comes, (other, k - step))
    pl.semaphore_wait(
        barrier,
        1 + 2 * goes_after.astype(jnp.int32) + 2 * comes.astype(jnp.int32)
        + goes.astype(jnp.int32) + comes_after.astype(jnp.int32),
    )

    def remote(source, target, send_sem, recv_sem, device):
        return pltpu.make_async_remote_copy(
            src_ref=source, dst_ref=target, send_sem=send_sem, recv_sem=recv_sem,
            device_id=device, device_id_type=MESH,
        )

    def when_do(condition, copies, action):
        @pl.when(condition)
        def _():
            for copy in copies:
                getattr(copy, action)()

    def near_copies(site, target, state, device, way):
        return [
            remote(source, sink, near_send.at[way, i], near_recv.at[site, i], device)
            for i, (source, sink) in enumerate([
                (pack_in, near_pack.at[site]),
                (states_in.at[0, target, 3, 0], near_blocks.at[site, 1]),
                (states_in.at[0, target, state, 0], near_blocks.at[site, 0]),
            ])
        ]

    def env_copy(site, c):
        span = pl.ds(*SPANS[c])
        source = env_in.at[core, 0, span] if site == 0 else env.at[1, span]
        return remote(
            source, near_env.at[site, span], env_send.at[site, c], env_recv.at[site, c], (core, k + step)
        )

    def got_copy(site, c):
        span = pl.ds(*SPANS[c])
        return remote(
            merged.at[site, span], got.at[site, span], got_send.at[site, c], got_recv.at[site, c],
            (core, k + step_after),
        )

    swaps = [
        remote(source, target, swap_send.at[i], swap_recv.at[i], (other, k))
        for i, (source, target) in enumerate(
            [(pack_in, pack.at[core]), (states_in.at[0, other, :, 0], blocks.at[core])]
        )
    ]
    near_same = near_copies(core, core, state_first, (core, k + step), 0)
    near_other = near_copies(core, other, state_after, (other, k + step_after), 1)
    for swap in swaps:
        swap.start()
    when_do(goes & (core == 0), near_same, "start")
    when_do(goes_after & (core == 0), near_other, "start")
    when_do(goes, [env_copy(0, c) for c in range(CHUNKS)], "start")
    when_do(goes & (core == 1), near_same, "start")
    when_do(goes_after & (core == 1), near_other, "start")

    proj[:, W] = jnp.zeros((2, BLK, 2 * BLK), BF)

    @pl.when(jnp.logical_not(comes))
    def _():
        near_blocks[...] = jnp.zeros_like(near_blocks)
        near_pack[...] = jnp.zeros_like(near_pack)
        near_env[...] = jnp.zeros_like(near_env)

    @pl.when(jnp.logical_not(comes_after))
    def _():
        got[...] = jnp.zeros_like(got)

    def prepare(q, coupling, block):
        spread = (lax.broadcasted_iota(jnp.int32, (W * SUB, SUB), 0) >> 4) == lax.broadcasted_iota(
            jnp.int32, (W * SUB, SUB), 1
        )
        spread = jnp.where(spread, 1.0, 0.0).astype(BF)
        widen = lax.broadcasted_iota(jnp.int32, (BLK, 256), 0) == (
            lax.broadcasted_iota(jnp.int32, (BLK, 256), 1) >> 4
        )
        widen = jnp.where(widen, 1.0, 0.0).astype(BF)
        same = (lax.broadcasted_iota(jnp.int32, (W * SUB, 256), 0) & 15) == (
            lax.broadcasted_iota(jnp.int32, (W * SUB, 256), 1) & 15
        )
        tall = jnp.dot(spread, coupling, preferred_element_type=F32).astype(BF)
        wide = jnp.dot(tall, widen, preferred_element_type=F32)
        kron[q] = jnp.where(same, wide, 0.0).astype(BF)
        joined[q // 2, :, (q % 2) * BLK:(q % 2 + 1) * BLK] = block
        turned[q] = block.astype(F32).T.astype(BF)

    def prepare_own(site):
        @pl.when(core == site)
        def _():
            own_blocks.wait()
            own_pack.wait()

        when_do(core != site, swaps, "wait_recv")
        prepare(0, pack[site, 0], blocks[site, 0])
        prepare(1, pack[site, state_after], blocks[site, state_after])

    def prepare_near(site):
        when_do(comes, near_copies(site, core, state_first, (core, k + step), 0), "wait_recv")
        prepare(2, near_pack[site, state_first], near_blocks[site, 0])
        prepare(3, near_pack[site, 3], near_blocks[site, 1])

    def project(half, source, c):
        low, many = SPANS[c]
        rows = source[low:low + many].reshape(many * BLK, BLK)
        product = jnp.dot(rows, joined[half], preferred_element_type=F32).astype(BF)
        proj[half, low:low + many] = product.reshape(many, BLK, 2 * BLK)

    def mix(site, q):
        half, lanes = q // 2, slice((q % 2) * BLK, (q % 2 + 1) * BLK)
        for i in range(BLK // (2 * SUB)):
            low, mid, high = 2 * i * SUB, (2 * i + 1) * SUB, (2 * i + 2) * SUB
            pair = jnp.concatenate(
                [proj[half, :, low:mid, lanes].reshape(256, BLK), proj[half, :, mid:high, lanes].reshape(256, BLK)],
                axis=1,
            )
            product = jnp.dot(kron[q], pair, preferred_element_type=F32).astype(BF)
            for v in range(W):
                mixed[low:mid, v * BLK:(v + 1) * BLK] = product[v * SUB:(v + 1) * SUB, :BLK]
                mixed[mid:high, v * BLK:(v + 1) * BLK] = product[v * SUB:(v + 1) * SUB, BLK:]
        for c, (low, many) in enumerate(SPANS):
            product = jnp.dot(
                turned[q], mixed[:, low * BLK:(low + many) * BLK], preferred_element_type=F32
            )
            for v in range(many):
                part = product[:, v * BLK:(v + 1) * BLK]
                if q == 3:
                    merged[site, low + v] = (part + parts[1, low + v].astype(F32)).astype(BF)
                else:
                    parts[q, low + v] = part.astype(BF)
            if q == 3:
                when_do(goes_after, [got_copy(site, c)], "start")

    def out_copies(site, c):
        span = pl.ds(*SPANS[c])
        source, target = env.at[site + 1, span], out.at[0, core, 0, span]
        local = pltpu.make_async_copy(source, target, out_sem.at[c])
        return local, remote(source, target, out_send.at[c], out_recv.at[c], (other, k))

    def combine(site, c):
        when_do(comes_after, [got_copy(site, c)], "wait_recv")
        size = pack[site, 4].astype(F32)[0:1]
        live = (lax.broadcasted_iota(jnp.int32, (BLK, BLK), 0).astype(F32) < size) & (
            lax.broadcasted_iota(jnp.int32, (BLK, BLK), 1).astype(F32) < size
        )
        low, many = SPANS[c]
        for v in range(low, low + many):
            total = parts[0, v].astype(F32) + parts[2, v].astype(F32) + got[site, v].astype(F32)
            env[site + 1, v] = jnp.where(live, total, 0.0).astype(BF)
        if site == 0:
            when_do(goes, [env_copy(1, c)], "start")
        local, across = out_copies(site, c)
        when_do(core == site, [local], "start")
        when_do(core != site, [across], "start")

    for site in range(2):
        prepare_own(site)
        if site == 1:
            prepare_near(site)
        for c in range(CHUNKS):
            if site == 0:
                own_env[c].wait()
            else:
                combine(0, c)
            project(0, env.at[site], c)
        mix(site, 1)
        if site == 0:
            prepare_near(site)
        for c in range(CHUNKS):
            when_do(comes, [env_copy(site, c)], "wait_recv")
            project(1, near_env.at[site], c)
        mix(site, 3)
        mix(site, 2)
        mix(site, 0)
    for c in range(CHUNKS):
        combine(1, c)

    for swap in swaps:
        swap.wait_send()
    when_do(goes, near_same, "wait_send")
    when_do(goes_after, near_other, "wait_send")
    for site in range(2):
        when_do(goes, [env_copy(site, c) for c in range(CHUNKS)], "wait_send")
        when_do(goes_after, [got_copy(site, c) for c in range(CHUNKS)], "wait_send")
    for site in range(2):
        for c in range(CHUNKS):
            local, across = out_copies(site, c)
            @pl.when(core == site)
            def _():
                local.wait()
                across.wait_recv()

            when_do(core != site, [across], "wait_send")


def on_device(env_first, states, mpo, block_rows, present):
    down_charge = lax.axis_index("sector") % QD
    inside = jnp.where(jnp.arange(4) >= 2, (down_charge < QD - 1).astype(F32), 1.0)
    keep = present[0, :, 0].astype(F32) * inside
    coupling = jnp.swapaxes(mpo[0], 1, 2).astype(F32) * keep[:, None, None]
    coupling = jnp.pad(coupling, ((0, 0), (0, SUB - W), (0, BLK - W)))
    size = jnp.broadcast_to(block_rows[0, 0].astype(F32), (1, SUB, BLK))
    pack = jnp.concatenate([coupling, size], axis=0).astype(BF)
    anywhere = pl.BlockSpec(memory_space=pl.ANY)
    return pl.pallas_call(
        kernel,
        out_shape=jax.ShapeDtypeStruct((1, 2, 1, W, BLK, BLK), BF),
        in_specs=[pl.BlockSpec(memory_space=pltpu.HBM)] * 2 + [anywhere],
        out_specs=anywhere,
        scratch_shapes=[
            pltpu.VMEM((3, W, BLK, BLK), BF),
            pltpu.VMEM((2, W, BLK, BLK), BF),
            pltpu.VMEM((2, 4, BLK, BLK), BF),
            pltpu.VMEM((2, 2, BLK, BLK), BF),
            pltpu.VMEM((2, 5, SUB, BLK), BF),
            pltpu.VMEM((2, 5, SUB, BLK), BF),
            pltpu.VMEM((2, BLK, 2 * BLK), BF),
            pltpu.VMEM((4, BLK, BLK), BF),
            pltpu.VMEM((4, W * SUB, 256), BF),
            pltpu.VMEM((2, W + 1, BLK, 2 * BLK), BF),
            pltpu.VMEM((BLK, W * BLK), BF),
            pltpu.VMEM((3, W, BLK, BLK), BF),
            pltpu.VMEM((2, W, BLK, BLK), BF),
            pltpu.VMEM((2, W, BLK, BLK), BF),
            pltpu.SemaphoreType.DMA((CHUNKS,)),
            pltpu.SemaphoreType.DMA((2,)),
            pltpu.SemaphoreType.DMA((2,)),
            pltpu.SemaphoreType.DMA((2,)),
            pltpu.SemaphoreType.DMA((2, 3)),
            pltpu.SemaphoreType.DMA((2, 3)),
            pltpu.SemaphoreType.DMA((2, CHUNKS)),
            pltpu.SemaphoreType.DMA((2, CHUNKS)),
            pltpu.SemaphoreType.DMA((2, CHUNKS)),
            pltpu.SemaphoreType.DMA((2, CHUNKS)),
            pltpu.SemaphoreType.DMA((CHUNKS,)),
            pltpu.SemaphoreType.DMA((CHUNKS,)),
            pltpu.SemaphoreType.DMA((CHUNKS,)),
        ],
        compiler_params=pltpu.CompilerParams(
            collective_id=0, has_side_effects=True, vmem_limit_bytes=48 * 1024 * 1024
        ),
    )(
        pltpu.with_memory_space_constraint(env_first, pltpu.HBM),
        pltpu.with_memory_space_constraint(states, pltpu.HBM),
        pack,
    )


def solution(mesh):
    placed = (
        P(None, "sector", None, None, None),
        P("chain", None, None, "sector", None, None),
        P("chain", None, None, None),
        P("chain", "sector"),
        P("chain", None, "sector"),
    )
    return jax.shard_map(
        on_device,
        mesh=mesh,
        in_specs=placed,
        out_specs=P("chain", None, "sector", None, None, None),
        check_vma=False,
    )
```
